512 devices in a mesh: tok: 8 (over z), row: 8 (over y_hi, core), col: 8 (over x, y_lo).
Axes of the slice: x: 4, y: 8 (y_hi: 4, y_lo: 2; y = y_hi * 2 + y_lo), z: 8, core: 2. Of those that a mesh axis runs over, the one named last changes fastest.
Arguments:
- activations: bfloat16 [2048, 8192], P('tok', 'row'), may hold values from -8 to 8
- gradients: bfloat16 [2048, 8192], P('tok', 'col'), may hold values from -8 to 8
- act_basis: bfloat16 [8192, 8192], P('row', ('tok', 'col')), may hold values from -1 to 1
- grad_basis: bfloat16 [8192, 8192], P('col', 'row'), may hold values from -1 to 1
- eigen_noise: float32 [8192, 8192], P('row', ('tok', 'col')), may hold values from -6 to 6
Outputs:
- scales: float32 [8192, 8192], P('row', ('tok', 'col'))
- output_shift: bfloat16 [2048, 8192], P('tok', 'col')
The draws below stay inside these ranges and needn't reach their ends.
All inputs are finite; a program needn't handle non-finite values.
Results may differ from the reference program's by a relative error of at most 0.0064.
Values may be sent and summed in bfloat16 or wider, within the bound.
No kernel may reach another device: no remote copies, remote signals or barrier semaphores. Data moves between devices by JAX's collectives and lax.ppermute only.
A program may use at most 64 MiB of HBM per device.

```python
import math
import jax
import jax.numpy as jnp
from jax import lax

D = 8192
TOKENS = 2048


def token_scale(key, salt):
    lower = math.log(0.9)
    upper = math.log(1.1)
    spread = jax.random.uniform(jax.random.fold_in(key, salt), (TOKENS, 1), jnp.float32, lower, upper)
    return jnp.exp(spread)


def column_scale(key):
    spread = jax.random.uniform(key, (1, D), jnp.float32, math.log(0.5), math.log(2.0))
    return jnp.exp(spread)


def unit_values(key, shape):
    return jnp.clip(jax.random.normal(key, shape, jnp.float32), -4.0, 4.0)


def draw_activations(key, part):
    values = unit_values(jax.random.fold_in(key, 21), (TOKENS, D))
    return (token_scale(key, 7) * values).astype(jnp.bfloat16)


def draw_gradients(key, part):
    values = unit_values(jax.random.fold_in(key, 22), (TOKENS, D))
    return (token_scale(key, 8) * values).astype(jnp.bfloat16)


def draw_act_basis(key, part):
    values = unit_values(jax.random.fold_in(key, 41), (D, D))
    factor = column_scale(jax.random.fold_in(key, 31))
    return (factor * values / math.sqrt(D)).astype(jnp.bfloat16)


def draw_grad_basis(key, part):
    values = unit_values(jax.random.fold_in(key, 42), (D, D))
    factor = column_scale(jax.random.fold_in(key, 32))
    return (factor * values / math.sqrt(D)).astype(jnp.bfloat16)


def shard_levels(key, extent, split, smallest, largest):
    factor_of = 1.0
    for dim, shards_of in split:
        draws = jax.random.uniform(jax.random.fold_in(jax.random.fold_in(key, 6), dim), (shards_of,), jnp.float32, smallest / len(split), largest / len(split))
        factor_of = factor_of * jnp.repeat(jnp.exp(draws), extent[dim] // shards_of).reshape((-1,) + (1,) * (len(extent) - 1 - dim))
    return factor_of


def noise(stream_key, extent, deviation, limit, cuts=(), kind=jnp.bfloat16):
    drawn = deviation * jax.random.normal(stream_key, extent, jnp.float32)
    if cuts:
        drawn = drawn * shard_levels(stream_key, extent, cuts, -0.22, 0.18)
    return jnp.clip(drawn, -limit, limit).astype(kind)


def setup_inputs(seed: int = 0) -> dict:
    seeds = jax.random.split(jax.random.key(seed), 6)
    return {
        "activations": draw_activations(jax.random.fold_in(seeds[5], 71), 0),
        "gradients": draw_gradients(jax.random.fold_in(seeds[5], 71), 0),
        "act_basis": draw_act_basis(jax.random.fold_in(seeds[5], 71), 0),
        "grad_basis": draw_grad_basis(jax.random.fold_in(seeds[5], 71), 0),
        "eigen_noise": noise(seeds[4], (D, D), 1.0, 6.0, ((0, 8), (1, 64)), jnp.float32),
    }


damping = 0.1

def contract(former, latter, former_dim, latter_dim):
    return lax.dot_general(former, latter, (((former_dim,), (latter_dim,)), ((), ())), preferred_element_type=jnp.float32)

def reference(activations, gradients, act_basis, grad_basis, eigen_noise):
    act_proj = contract(activations, act_basis, 1, 0)
    grad_proj = contract(gradients, grad_basis, 1, 0)
    act_sq = (act_proj * act_proj).astype(jnp.bfloat16)
    grad_sq = (grad_proj * grad_proj).astype(jnp.bfloat16)
    scales = contract(grad_sq, act_sq, 0, 0) / TOKENS
    scaled = (eigen_noise * lax.rsqrt(TOKENS * (scales + damping))).astype(jnp.bfloat16)
    act_half = act_proj.astype(jnp.bfloat16)
    hidden = contract(act_half, scaled, 1, 1).astype(jnp.bfloat16)
    output_shift = contract(hidden, grad_basis, 1, 1).astype(jnp.bfloat16)
    return (scales, output_shift)
```

```python
import jax
import jax.numpy as jnp
from jax import lax
from jax.sharding import Mesh, PartitionSpec as P

damping = 0.1
narrow = jnp.bfloat16
wide = jnp.float32
row = ("yh", "core")
col = ("x", "yl")


def contract(former, latter, former_dim, latter_dim):
    return lax.dot_general(
        former,
        latter,
        (((former_dim,), (latter_dim,)), ((), ())),
        preferred_element_type=wide,
    )


def exchange(blocks, axes):
    return lax.all_to_all(blocks, axes, 0, 0, tiled=True)


def spread(block, axes):
    members = lax.axis_size(axes)
    copies = jnp.broadcast_to(block[None], (members, *block.shape))
    return exchange(copies.reshape(members * block.shape[0], *block.shape[1:]), axes)


def scatter_sum(partial, axes):
    members = lax.axis_size(axes)
    parts = exchange(partial.astype(narrow), axes)
    parts = parts.reshape(members, parts.shape[0] // members, *parts.shape[1:])
    return jnp.sum(parts.astype(wide), axis=0)


def shards(activations, gradients, act_basis, grad_basis, eigen_noise):
    token_count = activations.shape[0] * lax.axis_size("tok")
    slab = activations.shape[0] // lax.axis_size("x")

    grad_proj = scatter_sum(contract(gradients, grad_basis, 1, 0), col)
    grad_sq = spread((grad_proj * grad_proj).astype(narrow), ("tok", "yl"))

    own_rows = lax.dynamic_slice_in_dim(activations, lax.axis_index("x") * slab, slab, 0)
    act_rows = spread(own_rows, "tok")
    basis_t = spread(act_basis.T, "x")
    act_proj = scatter_sum(contract(act_rows, basis_t, 1, 1), row)
    act_half = lax.all_gather(act_proj.astype(narrow), row, axis=0, tiled=True)
    act_wide = act_half.astype(wide)
    act_sq = (act_wide * act_wide).astype(narrow)

    scales_t = scatter_sum(contract(act_sq, grad_sq, 0, 0), "x") / token_count
    scaled_t = (eigen_noise.T * lax.rsqrt(token_count * (scales_t + damping))).astype(narrow)
    widened_t = spread(scaled_t, "x")

    hidden = scatter_sum(contract(act_half, widened_t, 1, 0), ("tok", "yl")).astype(narrow)
    hidden = spread(hidden, col)
    shift = scatter_sum(contract(hidden, grad_basis, 1, 1), row).astype(narrow)
    output_shift = lax.all_gather(shift, row, axis=0, tiled=True)
    return (scales_t.T, output_shift)


def solution(mesh):
    fine = Mesh(mesh.devices.reshape(8, 4, 2, 4, 2), ("tok", "yh", "core", "x", "yl"))
    in_specs = (
        P("tok", row),
        P("tok", col),
        P(row, ("tok", *col)),
        P(col, row),
        P(row, ("tok", *col)),
    )
    out_specs = (P(row, ("tok", *col)), P("tok", col))
    return jax.shard_map(shards, mesh=fine, in_specs=in_specs, out_specs=out_specs, check_vma=False)
```

```python
import jax
import jax.numpy as jnp
from jax import lax
from jax.sharding import Mesh, PartitionSpec as P

damping = 0.1
narrow = jnp.bfloat16
wide = jnp.float32
row = ("yh", "core")
col = ("x", "yl")


def contract(former, latter, former_dim, latter_dim):
    return lax.dot_general(
        former,
        latter,
        (((former_dim,), (latter_dim,)), ((), ())),
        preferred_element_type=wide,
    )


def exchange(blocks, axes):
    return lax.all_to_all(blocks, axes, 0, 0, tiled=True)


def spread(block, axes):
    members = lax.axis_size(axes)
    copies = jnp.broadcast_to(block[None], (members, *block.shape))
    return exchange(copies.reshape(members * block.shape[0], *block.shape[1:]), axes)


def scatter_sum(partial, axes):
    members = lax.axis_size(axes)
    parts = exchange(partial.astype(narrow), axes)
    parts = parts.reshape(members, parts.shape[0] // members, *parts.shape[1:])
    return jnp.sum(parts.astype(wide), axis=0)


def pick(blocks, index, axis):
    return lax.dynamic_index_in_dim(blocks, index, axis, keepdims=False)


def shifted(block, axis, step):
    members = lax.axis_size(axis)
    return lax.ppermute(block, axis, [(i, (i + step) % members) for i in range(members)])


def pair_sum(partial, axis):
    half = partial.reshape(4, 2, partial.shape[0] // 8, partial.shape[1])
    mine = lax.axis_index(axis)
    theirs = shifted(pick(half, 1 - mine, 1).astype(narrow), axis, 1)
    return pick(half, mine, 1) + theirs.astype(wide)


def ring_sum(halves, axis):
    mine = lax.axis_index(axis)
    sent = halves.astype(narrow)
    total = pick(halves, mine, 0)
    for step in range(1, 4):
        total = total + shifted(pick(sent, (mine + step) % 4, 0), axis, step).astype(wide)
    return total


def spread_by_permutes(block, axis):
    members = lax.axis_size(axis)
    mine = lax.axis_index(axis)
    gathered = jnp.zeros((members, *block.shape), block.dtype)
    for step in range(members):
        piece = shifted(block, axis, step) if step else block
        gathered = lax.dynamic_update_index_in_dim(gathered, piece, (mine - step) % members, 0)
    return gathered.reshape(members * block.shape[0], *block.shape[1:])


def shards(activations, gradients, act_basis, grad_basis, eigen_noise):
    token_count = activations.shape[0] * lax.axis_size("tok")
    slab = activations.shape[0] // lax.axis_size("x")

    own_rows = lax.dynamic_slice_in_dim(activations, lax.axis_index("x") * slab, slab, 0)
    act_rows = spread(own_rows, "tok")
    basis_t = spread_by_permutes(act_basis.T, "x")

    grad_proj = ring_sum(pair_sum(contract(gradients, grad_basis, 1, 0), "yl"), "x")
    grad_sq = spread((grad_proj * grad_proj).astype(narrow), ("tok", "yl"))

    act_proj = ring_sum(pair_sum(contract(act_rows, basis_t, 1, 1), "core"), "yh")
    act_half = lax.all_gather(act_proj.astype(narrow), row, axis=0, tiled=True)
    act_wide = act_half.astype(wide)
    act_sq = (act_wide * act_wide).astype(narrow)

    scales_t = scatter_sum(contract(act_sq, grad_sq, 0, 0), "x") / token_count
    scaled_t = (eigen_noise.T * lax.rsqrt(token_count * (scales_t + damping))).astype(narrow)
    widened_t = spread(scaled_t, "x")

    hidden = scatter_sum(contract(act_half, widened_t, 1, 0), ("tok", "yl")).astype(narrow)
    hidden = spread(hidden, col)
    halves = pair_sum(contract(hidden, grad_basis, 1, 1), "core")
    shift = scatter_sum(halves, "yh")[0].astype(narrow)
    output_shift = lax.all_gather(shift, row, axis=0, tiled=True)
    return (scales_t.T, output_shift)


def solution(mesh):
    fine = Mesh(mesh.devices.reshape(8, 4, 2, 4, 2), ("tok", "yh", "core", "x", "yl"))
    in_specs = (
        P("tok", row),
        P("tok", col),
        P(row, ("tok", *col)),
        P(col, row),
        P(row, ("tok", *col)),
    )
    out_specs = (P(row, ("tok", *col)), P("tok", col))
    return jax.shard_map(shards, mesh=fine, in_specs=in_specs, out_specs=out_specs, check_vma=False)
```

```python
import jax
import jax.numpy as jnp
from jax import lax
from jax.sharding import Mesh, PartitionSpec as P

damping = 0.1
narrow = jnp.bfloat16
wide = jnp.float32
row = ("yh", "core")
col = ("x", "yl")


def contract(former, latter, former_dim, latter_dim):
    return lax.dot_general(
        former,
        latter,
        (((former_dim,), (latter_dim,)), ((), ())),
        preferred_element_type=wide,
    )


def exchange(blocks, axes):
    return lax.all_to_all(blocks, axes, 0, 0, tiled=True)


def spread(block, axes):
    members = lax.axis_size(axes)
    copies = jnp.broadcast_to(block[None], (members, *block.shape))
    return exchange(copies.reshape(members * block.shape[0], *block.shape[1:]), axes)


def scatter_sum(partial, axes):
    members = lax.axis_size(axes)
    parts = exchange(partial.astype(narrow), axes)
    parts = parts.reshape(members, parts.shape[0] // members, *parts.shape[1:])
    return jnp.sum(parts.astype(wide), axis=0)


def pick(blocks, index, axis):
    return lax.dynamic_index_in_dim(blocks, index, axis, keepdims=False)


def shifted(block, axis, step):
    members = lax.axis_size(axis)
    return lax.ppermute(block, axis, [(i, (i + step) % members) for i in range(members)])


def pair_sum(rows, weights, weights_dim, axis):
    half = rows.reshape(4, 2, rows.shape[0] // 8, rows.shape[1])
    mine = lax.axis_index(axis)

    def product(which):
        return contract(pick(half, which, 1), weights, 2, weights_dim)

    theirs = shifted(product(1 - mine).astype(narrow), axis, 1)
    return lax.optimization_barrier(product(mine)) + theirs.astype(wide)


def ring_sum(halves, axis):
    mine = lax.axis_index(axis)
    sent = halves.astype(narrow)
    total = pick(halves, mine, 0)
    for step in range(1, 4):
        total = total + shifted(pick(sent, (mine + step) % 4, 0), axis, step).astype(wide)
    return total


def gather_back(block, axis):
    return [block] + [shifted(block, axis, step) for step in range(1, lax.axis_size(axis))]


def sum_back(blocks, axis):
    total = lax.optimization_barrier(blocks[0]).astype(wide)
    for step in range(1, lax.axis_size(axis)):
        total = total + shifted(blocks[step], axis, -step).astype(wide)
    return total


def plan(activations, gradients, act_basis, grad_basis, eigen_noise):
    token_count = activations.shape[0] * lax.axis_size("tok")
    slab = activations.shape[0] // lax.axis_size("x")

    own_rows = lax.dynamic_slice_in_dim(activations, lax.axis_index("x") * slab, slab, 0)
    act_rows = spread(own_rows, "tok")
    basis_t = jnp.concatenate(gather_back(act_basis.T, "x"), axis=0)

    grad_halves = pair_sum(gradients, grad_basis, 0, "yl")
    grad_proj = ring_sum(grad_halves, "x")
    grad_sq = (grad_proj * grad_proj).astype(narrow)

    act_halves = pair_sum(act_rows, basis_t, 1, "core")
    act_proj = ring_sum(act_halves, "yh")
    grad_sq = spread(grad_sq, ("tok", "yl"))
    act_half = lax.all_gather(act_proj.astype(narrow), row, axis=0, tiled=True)

    act_parts = jnp.split(act_half, 4, axis=1)

    def scales_part(part):
        act_wide = part.astype(wide)
        return contract((act_wide * act_wide).astype(narrow), grad_sq, 0, 0).astype(narrow)

    scales_t = sum_back([scales_part(part) for part in act_parts], "x") / token_count
    scaled_t = (eigen_noise.T * lax.rsqrt(token_count * (scales_t + damping))).astype(narrow)
    widened_t = gather_back(scaled_t, "x")

    hidden_part = sum(contract(a, w, 1, 0) for a, w in zip(act_parts, widened_t))
    hidden = scatter_sum(hidden_part, ("tok", "yl")).astype(narrow)
    hidden = spread(hidden, col)
    halves = pair_sum(hidden, grad_basis, 1, "core")
    shift = scatter_sum(halves, "yh")[0].astype(narrow)
    output_shift = lax.all_gather(shift, row, axis=0, tiled=True)
    return (scales_t.T, output_shift)


def solution(mesh):
    fine = Mesh(mesh.devices.reshape(8, 4, 2, 4, 2), ("tok", "yh", "core", "x", "yl"))
    in_specs = (
        P("tok", row),
        P("tok", col),
        P(row, ("tok", *col)),
        P(col, row),
        P(row, ("tok", *col)),
    )
    out_specs = (P(row, ("tok", *col)), P("tok", col))
    return jax.shard_map(plan, mesh=fine, in_specs=in_specs, out_specs=out_specs, check_vma=False)
```

```python
import jax
import jax.numpy as jnp
from jax import lax
from jax.sharding import Mesh, PartitionSpec as P

damping = 0.1
narrow = jnp.bfloat16
wide = jnp.float32
row = ("yh", "core")
col = ("x", "yl")


def contract(former, latter, former_dim, latter_dim):
    return lax.dot_general(
        former,
        latter,
        (((former_dim,), (latter_dim,)), ((), ())),
        preferred_element_type=wide,
    )


def exchange(blocks, axes):
    return lax.all_to_all(blocks, axes, 0, 0, tiled=True)


def spread(block, axes):
    members = lax.axis_size(axes)
    copies = jnp.broadcast_to(block[None], (members, *block.shape))
    return exchange(copies.reshape(members * block.shape[0], *block.shape[1:]), axes)


def scatter_sum(partial, axes):
    members = lax.axis_size(axes)
    parts = exchange(partial.astype(narrow), axes)
    parts = parts.reshape(members, parts.shape[0] // members, *parts.shape[1:])
    return jnp.sum(parts.astype(wide), axis=0)


def pick(blocks, index, axis):
    return lax.dynamic_index_in_dim(blocks, index, axis, keepdims=False)


def shifted(block, axis, step):
    members = lax.axis_size(axis)
    return lax.ppermute(block, axis, [(i, (i + step) % members) for i in range(members)])


def pair_sum(partial, axis):
    half = partial.reshape(4, 2, partial.shape[0] // 8, partial.shape[1])
    mine = lax.axis_index(axis)
    theirs = shifted(pick(half, 1 - mine, 1).astype(narrow), axis, 1)
    return pick(half, mine, 1) + theirs.astype(wide)


def ring_sum(halves, axis):
    mine = lax.axis_index(axis)
    sent = halves.astype(narrow)
    total = pick(halves, mine, 0)
    for step in range(1, 4):
        total = total + shifted(pick(sent, (mine + step) % 4, 0), axis, step).astype(wide)
    return total


def gather_by_permutes(block, axis):
    members = lax.axis_size(axis)
    mine = lax.axis_index(axis)
    behind = [block] + [shifted(block, axis, step) for step in range(1, members)]
    placed = [lax.select_n((mine - place) % members, *behind) for place in range(members)]
    return lax.optimization_barrier(jnp.concatenate(placed, axis=0))


def plan(activations, gradients, act_basis, grad_basis, eigen_noise):
    token_count = activations.shape[0] * lax.axis_size("tok")
    slab = activations.shape[0] // lax.axis_size("x")

    own_rows = lax.dynamic_slice_in_dim(activations, lax.axis_index("x") * slab, slab, 0)
    act_rows = spread(own_rows, "tok")
    basis_t = gather_by_permutes(act_basis.T, "x")

    grad_part = contract(gradients, grad_basis, 1, 0)
    grad_half = ring_sum(grad_part.reshape(4, slab, grad_part.shape[1]), "x")
    grad_proj = grad_half + shifted(grad_half.astype(narrow), "yl", 1).astype(wide)
    grad_sq = (grad_proj * grad_proj).astype(narrow)

    act_halves = pair_sum(contract(act_rows, basis_t, 1, 1), "core")
    act_proj = ring_sum(act_halves, "yh")
    grad_sq = spread(grad_sq, "tok")
    act_half = lax.all_gather(act_proj.astype(narrow), row, axis=0, tiled=True)
    act_wide = act_half.astype(wide)
    act_sq = (act_wide * act_wide).astype(narrow)

    scales_t = scatter_sum(contract(act_sq, grad_sq, 0, 0), "x") / token_count
    scaled_t = (eigen_noise.T * lax.rsqrt(token_count * (scales_t + damping))).astype(narrow)
    widened_t = spread(scaled_t, "x")

    hidden = scatter_sum(contract(act_half, widened_t, 1, 0), ("tok", "yl")).astype(narrow)
    hidden = spread(hidden, col)
    halves = pair_sum(contract(hidden, grad_basis, 1, 1), "core")
    shift = scatter_sum(halves, "yh")[0].astype(narrow)
    output_shift = lax.all_gather(shift, row, axis=0, tiled=True)
    return (scales_t.T, output_shift)


def solution(mesh):
    fine = Mesh(mesh.devices.reshape(8, 4, 2, 4, 2), ("tok", "yh", "core", "x", "yl"))
    in_specs = (
        P("tok", row),
        P("tok", col),
        P(row, ("tok", *col)),
        P(col, row),
        P(row, ("tok", *col)),
    )
    out_specs = (P(row, ("tok", *col)), P("tok", col))
    return jax.shard_map(plan, mesh=fine, in_specs=in_specs, out_specs=out_specs, check_vma=False)
```

```python
import jax
import jax.numpy as jnp
from jax import lax
from jax.experimental.layout import Layout, with_layout_constraint
from jax.sharding import Mesh, PartitionSpec as P

damping = 0.1
narrow = jnp.bfloat16
wide = jnp.float32
row = ("yh", "core")
col = ("x", "yl")


def contract(former, latter, former_dim, latter_dim):
    return lax.dot_general(
        former,
        latter,
        (((former_dim,), (latter_dim,)), ((), ())),
        preferred_element_type=wide,
    )


def exchange(blocks, axes):
    return lax.all_to_all(blocks, axes, 0, 0, tiled=True)


def spread(block, axes):
    members = lax.axis_size(axes)
    copies = jnp.broadcast_to(block[None], (members, *block.shape))
    return exchange(copies.reshape(members * block.shape[0], *block.shape[1:]), axes)


def scatter_sum(partial, axes):
    members = lax.axis_size(axes)
    parts = exchange(partial.astype(narrow), axes)
    parts = parts.reshape(members, parts.shape[0] // members, *parts.shape[1:])
    return jnp.sum(parts.astype(wide), axis=0)


def pick(blocks, index, axis):
    return lax.dynamic_index_in_dim(blocks, index, axis, keepdims=False)


def shifted(block, axis, step):
    members = lax.axis_size(axis)
    return lax.ppermute(block, axis, [(i, (i + step) % members) for i in range(members)])


def pair_sum(partial, axis):
    half = partial.reshape(4, 2, partial.shape[0] // 8, partial.shape[1])
    mine = lax.axis_index(axis)
    sent, kept = lax.optimization_barrier((pick(half, 1 - mine, 1).astype(narrow), pick(half, mine, 1)))
    return kept + shifted(sent, axis, 1).astype(wide)


def ring_sum(halves, axis):
    mine = lax.axis_index(axis)
    sent = halves.astype(narrow)
    total = pick(halves, mine, 0)
    for step in range(1, 4):
        total = total + shifted(pick(sent, (mine + step) % 4, 0), axis, step).astype(wide)
    return total


def gather_and_ring_sum(block, halves, axis):
    members = lax.axis_size(axis)
    mine = lax.axis_index(axis)
    depth = block.shape[0]
    sent = [pick(halves, (mine + step) % members, 0).astype(narrow) for step in range(1, members)]
    sent = [jnp.concatenate((block, part), axis=0) for part in sent]
    got = [shifted(message, axis, step) for step, message in enumerate(sent, 1)]
    total = pick(halves, mine, 0)
    for message in got:
        total = total + message[depth:].astype(wide)
    behind = [block] + [message[:depth] for message in got]
    placed = [lax.select_n((mine - place) % members, *behind) for place in range(members)]
    return lax.optimization_barrier(jnp.concatenate(placed, axis=0)), total


def plan(activations, gradients, act_basis, grad_basis, eigen_noise):
    token_count = activations.shape[0] * lax.axis_size("tok")
    slab = activations.shape[0] // lax.axis_size("x")

    own_rows = lax.dynamic_slice_in_dim(activations, lax.axis_index("x") * slab, slab, 0)
    act_rows = spread(own_rows, "tok")
    grad_part = contract(gradients, grad_basis, 1, 0)
    grad_part = grad_part.reshape(-1, slab, grad_part.shape[1])
    basis_t, grad_half = gather_and_ring_sum(with_layout_constraint(act_basis.T, Layout((0, 1))), grad_part, "x")
    grad_proj = grad_half + shifted(grad_half.astype(narrow), "yl", 1).astype(wide)
    grad_sq = (grad_proj * grad_proj).astype(narrow)

    act_halves = pair_sum(contract(act_rows, basis_t, 1, 1), "core")
    act_proj = ring_sum(act_halves, "yh")
    grad_sq = spread(grad_sq, "tok")
    act_half = lax.all_gather(act_proj.astype(narrow), row, axis=0, tiled=True)
    act_wide = act_half.astype(wide)
    act_sq = (act_wide * act_wide).astype(narrow)

    scales_t = scatter_sum(contract(act_sq, grad_sq, 0, 0), "x") / token_count
    scaled_t = (eigen_noise.T * lax.rsqrt(token_count * (scales_t + damping))).astype(narrow)
    widened_t = spread(scaled_t, "x")

    hidden = scatter_sum(contract(act_half, widened_t, 1, 0), ("tok", "yl")).astype(narrow)
    hidden = spread(hidden, col)
    halves = pair_sum(contract(hidden, grad_basis, 1, 1), "core")
    shift = scatter_sum(halves, "yh")[0].astype(narrow)
    output_shift = lax.all_gather(shift, row, axis=0, tiled=True)
    return (scales_t.T, output_shift)


def solution(mesh):
    fine = Mesh(mesh.devices.reshape(8, 4, 2, 4, 2), ("tok", "yh", "core", "x", "yl"))
    in_specs = (
        P("tok", row),
        P("tok", col),
        P(row, ("tok", *col)),
        P(col, row),
        P(row, ("tok", *col)),
    )
    out_specs = (P(row, ("tok", *col)), P("tok", col))
    return jax.shard_map(plan, mesh=fine, in_specs=in_specs, out_specs=out_specs, check_vma=False)
```

```python
import jax
import jax.numpy as jnp
from jax import lax
from jax.experimental.layout import Layout, with_layout_constraint
from jax.sharding import Mesh, PartitionSpec as P

damping = 0.1
narrow = jnp.bfloat16
wide = jnp.float32
row = ("yh", "core")
col = ("x", "yl")


def contract(former, latter, former_dim, latter_dim):
    return lax.dot_general(
        former,
        latter,
        (((former_dim,), (latter_dim,)), ((), ())),
        preferred_element_type=wide,
    )


def exchange(blocks, axes):
    return lax.all_to_all(blocks, axes, 0, 0, tiled=True)


def spread(block, axes):
    members = lax.axis_size(axes)
    copies = jnp.broadcast_to(block[None], (members, *block.shape))
    return exchange(copies.reshape(members * block.shape[0], *block.shape[1:]), axes)


def scatter_sum(partial, axes):
    members = lax.axis_size(axes)
    parts = exchange(partial.astype(narrow), axes)
    parts = parts.reshape(members, parts.shape[0] // members, *parts.shape[1:])
    return jnp.sum(parts.astype(wide), axis=0)


def pick(blocks, index, axis):
    return lax.dynamic_index_in_dim(blocks, index, axis, keepdims=False)


def shifted(block, axis, step):
    members = lax.axis_size(axis)
    return lax.ppermute(block, axis, [(i, (i + step) % members) for i in range(members)])


def pair_sum(partial, axis):
    half = partial.reshape(4, 2, partial.shape[0] // 8, partial.shape[1])
    mine = lax.axis_index(axis)
    sent, kept = lax.optimization_barrier((pick(half, 1 - mine, 1).astype(narrow), pick(half, mine, 1)))
    return kept + shifted(sent, axis, 1).astype(wide)


def ring_sum(halves, axis):
    mine = lax.axis_index(axis)
    sent = halves.astype(narrow)
    total = pick(halves, mine, 0)
    for step in range(1, 4):
        total = total + shifted(pick(sent, (mine + step) % 4, 0), axis, step).astype(wide)
    return total


def gather_and_ring_sum(block, halves, axis):
    members = lax.axis_size(axis)
    mine = lax.axis_index(axis)
    depth = block.shape[0]
    sent = [pick(halves, (mine + step) % members, 0).astype(narrow) for step in range(1, members)]
    sent = [jnp.concatenate((block, part), axis=0) for part in sent]
    got = [shifted(message, axis, step) for step, message in enumerate(sent, 1)]
    total = pick(halves, mine, 0)
    for message in got:
        total = total + message[depth:].astype(wide)
    return jnp.concatenate([block] + [message[:depth] for message in got], axis=0), total


def placed(columns, axis):
    members = lax.axis_size(axis)
    mine = lax.axis_index(axis)
    behind = jnp.split(columns, members, axis=1)
    return jnp.concatenate([lax.select_n((mine - place) % members, *behind) for place in range(members)], axis=1)


def plan(activations, gradients, act_basis, grad_basis, eigen_noise):
    token_count = activations.shape[0] * lax.axis_size("tok")
    slab = activations.shape[0] // lax.axis_size("x")

    own_rows = lax.dynamic_slice_in_dim(activations, lax.axis_index("x") * slab, slab, 0)
    act_rows = spread(own_rows, "tok")
    grad_part = contract(gradients, grad_basis, 1, 0)
    grad_part = grad_part.reshape(-1, slab, grad_part.shape[1])
    basis_t, grad_half = gather_and_ring_sum(with_layout_constraint(act_basis.T, Layout((0, 1))), grad_part, "x")
    grad_proj = grad_half + shifted(grad_half.astype(narrow), "yl", 1).astype(wide)
    grad_sq = (grad_proj * grad_proj).astype(narrow)

    act_halves = pair_sum(contract(act_rows, basis_t, 1, 1), "core")
    act_proj = ring_sum(act_halves, "yh")
    grad_sq = spread(grad_sq, "tok")
    act_half = lax.all_gather(placed(act_proj.astype(narrow), "x"), row, axis=0, tiled=True)
    own_basis, act_half = lax.optimization_barrier((grad_basis, act_half))
    their_basis = shifted(own_basis, "core", 1)
    act_wide = act_half.astype(wide)
    act_sq = (act_wide * act_wide).astype(narrow)

    scales_t = scatter_sum(contract(act_sq, grad_sq, 0, 0), "x") / token_count
    scaled_t = (eigen_noise.T * lax.rsqrt(token_count * (scales_t + damping))).astype(narrow)
    widened_t = spread(scaled_t, "x")

    parts = exchange(contract(act_half, widened_t, 1, 0).astype(narrow), ("tok", "core", "yl"))
    parts = parts.reshape(8, 2, 2, parts.shape[0] // 32, parts.shape[1])
    hidden = jnp.sum(parts.astype(wide), axis=(0, 2)).astype(narrow)
    mine = lax.axis_index("core")
    hidden = jnp.concatenate((pick(hidden, mine, 0), pick(hidden, 1 - mine, 0)), axis=1)
    hidden = spread(hidden, col)
    depth = grad_basis.shape[1]
    shift_part = contract(hidden[:, :depth], grad_basis, 1, 1) + contract(hidden[:, depth:], their_basis, 1, 1)
    shift = scatter_sum(shift_part, "yh").astype(narrow)
    output_shift = lax.all_gather(shift, row, axis=0, tiled=True)
    return (scales_t.T, output_shift)


def solution(mesh):
    fine = Mesh(mesh.devices.reshape(8, 4, 2, 4, 2), ("tok", "yh", "core", "x", "yl"))
    in_specs = (
        P("tok", row),
        P("tok", col),
        P(row, ("tok", *col)),
        P(col, row),
        P(row, ("tok", *col)),
    )
    out_specs = (P(row, ("tok", *col)), P("tok", col))
    return jax.shard_map(plan, mesh=fine, in_specs=in_specs, out_specs=out_specs, check_vma=False)
```

```python
import jax
import jax.numpy as jnp
from jax import lax
from jax.sharding import Mesh, PartitionSpec as P

damping = 0.1
narrow = jnp.bfloat16
wide = jnp.float32
row = ("yh", "core")
col = ("x", "yl")


def contract(former, latter, former_dim, latter_dim):
    return lax.dot_general(
        former,
        latter,
        (((former_dim,), (latter_dim,)), ((), ())),
        preferred_element_type=wide,
    )


def exchange(blocks, axes):
    return lax.all_to_all(blocks, axes, 0, 0, tiled=True)


def spread(block, axes):
    members = lax.axis_size(axes)
    copies = jnp.broadcast_to(block[None], (members, *block.shape))
    return exchange(copies.reshape(members * block.shape[0], *block.shape[1:]), axes)


def scatter_sum(partial, axes):
    members = lax.axis_size(axes)
    parts = exchange(partial.astype(narrow), axes)
    parts = parts.reshape(members, parts.shape[0] // members, *parts.shape[1:])
    return jnp.sum(parts.astype(wide), axis=0)


def pick(blocks, index, axis):
    return lax.dynamic_index_in_dim(blocks, index, axis, keepdims=False)


def shifted(block, axis, step):
    members = lax.axis_size(axis)
    return lax.ppermute(block, axis, [(i, (i + step) % members) for i in range(members)])


def pair_sum(partial, axis):
    half = partial.reshape(4, 2, partial.shape[0] // 8, partial.shape[1])
    mine = lax.axis_index(axis)
    sent, kept = lax.optimization_barrier((pick(half, 1 - mine, 1).astype(narrow), pick(half, mine, 1)))
    return kept + pick(lax.all_gather(sent, axis), 1 - mine, 0).astype(wide)


def ring_sum(blocks, axis):
    mine = lax.axis_index(axis)
    members = lax.axis_size(axis)
    sent = blocks.astype(narrow)
    total = pick(blocks, mine, 0)
    for step in range(1, members):
        total = total + shifted(pick(sent, (mine + step) % members, 0), axis, step).astype(wide)
    return total


def plan(activations, gradients, act_basis, grad_basis, eigen_noise):
    token_count = activations.shape[0] * lax.axis_size("tok")
    slab = activations.shape[0] // lax.axis_size("x")

    own_rows = lax.dynamic_slice_in_dim(activations, lax.axis_index("x") * slab, slab, 0)
    act_rows = spread(own_rows, "tok")
    grad_part = contract(gradients, grad_basis, 1, 0)
    grad_part = grad_part.reshape(-1, slab, grad_part.shape[1])
    basis = lax.all_gather(act_basis, "x", axis=1, tiled=True)
    grad_half = ring_sum(grad_part, "x")
    grad_proj = grad_half + shifted(grad_half.astype(narrow), "yl", 1).astype(wide)
    grad_sq = (grad_proj * grad_proj).astype(narrow)

    act_halves = pair_sum(contract(act_rows, basis, 1, 0), "core")
    act_proj = scatter_sum(act_halves, "yh")[0]
    grad_sq = lax.all_gather(grad_sq, "tok", axis=0, tiled=True)
    act_half = lax.all_gather(act_proj.astype(narrow), row, axis=0, tiled=True)
    act_wide = act_half.astype(wide)
    act_sq = (act_wide * act_wide).astype(narrow)

    scales_t = scatter_sum(contract(act_sq, grad_sq, 0, 0), "x") / token_count
    scaled_t = (eigen_noise.T * lax.rsqrt(token_count * (scales_t + damping))).astype(narrow)
    widened_t = spread(scaled_t, "x")

    hidden = scatter_sum(contract(act_half, widened_t, 1, 0), ("tok", "yl")).astype(narrow)
    hidden = spread(hidden, col)
    halves = pair_sum(contract(hidden, grad_basis, 1, 1), "core")
    shift = scatter_sum(halves, "yh")[0].astype(narrow)
    output_shift = lax.all_gather(shift, row, axis=0, tiled=True)
    return (scales_t.T, output_shift)


def solution(mesh):
    fine = Mesh(mesh.devices.reshape(8, 4, 2, 4, 2), ("tok", "yh", "core", "x", "yl"))
    in_specs = (
        P("tok", row),
        P("tok", col),
        P(row, ("tok", *col)),
        P(col, row),
        P(row, ("tok", *col)),
    )
    out_specs = (P(row, ("tok", *col)), P("tok", col))
    return jax.shard_map(plan, mesh=fine, in_specs=in_specs, out_specs=out_specs, check_vma=False)
```

```python
import jax
import jax.numpy as jnp
from jax import lax
from jax.sharding import Mesh, PartitionSpec as P

damping = 0.1
narrow = jnp.bfloat16
wide = jnp.float32
row = ("yh", "core")
col = ("x", "yl")


def contract(former, latter, former_dim, latter_dim):
    return lax.dot_general(
        former,
        latter,
        (((former_dim,), (latter_dim,)), ((), ())),
        preferred_element_type=wide,
    )


def exchange(blocks, axes):
    return lax.all_to_all(blocks, axes, 0, 0, tiled=True)


def spread(block, axes):
    members = lax.axis_size(axes)
    copies = jnp.broadcast_to(block[None], (members, *block.shape))
    return exchange(copies.reshape(members * block.shape[0], *block.shape[1:]), axes)


def scatter_sum(partial, axes):
    members = lax.axis_size(axes)
    parts = exchange(partial.astype(narrow), axes)
    parts = parts.reshape(members, parts.shape[0] // members, *parts.shape[1:])
    return jnp.sum(parts.astype(wide), axis=0)


def pick(blocks, index, axis):
    return lax.dynamic_index_in_dim(blocks, index, axis, keepdims=False)


def shifted(block, axis, step):
    members = lax.axis_size(axis)
    return lax.ppermute(block, axis, [(i, (i + step) % members) for i in range(members)])


def pair_sum(partial, axis):
    half = partial.reshape(4, 2, partial.shape[0] // 8, partial.shape[1])
    mine = lax.axis_index(axis)
    sent, kept = lax.optimization_barrier((pick(half, 1 - mine, 1).astype(narrow), pick(half, mine, 1)))
    return kept + pick(lax.all_gather(sent, axis), 1 - mine, 0).astype(wide)


def ring_sum(blocks, axis):
    mine = lax.axis_index(axis)
    members = lax.axis_size(axis)
    total = pick(blocks, mine, 0).astype(wide)
    for step in sorted(range(1, members), key=lambda step: abs(2 * step - members)):
        total = total + shifted(pick(blocks, (mine + step) % members, 0), axis, step).astype(wide)
    return total


def plan(activations, gradients, act_basis, grad_basis, eigen_noise):
    token_count = activations.shape[0] * lax.axis_size("tok")
    slab = activations.shape[0] // lax.axis_size("x")

    own_rows = lax.dynamic_slice_in_dim(activations, lax.axis_index("x") * slab, slab, 0)
    act_rows = spread(own_rows, "tok")
    grad_part = contract(gradients, grad_basis, 1, 0).astype(narrow)
    grad_part = grad_part.reshape(-1, slab, grad_part.shape[1])
    basis = lax.all_gather(act_basis, "x", axis=1, tiled=True)
    grad_half = ring_sum(grad_part, "x")
    grad_proj = grad_half + shifted(grad_half.astype(narrow), "yl", 1).astype(wide)
    grad_sq = (grad_proj * grad_proj).astype(narrow)

    act_halves = pair_sum(contract(act_rows, basis, 1, 0), "core")
    act_proj = scatter_sum(act_halves, "yh")[0]
    grad_sq = lax.all_gather(grad_sq, "tok", axis=0, tiled=True)
    act_half = lax.all_gather(act_proj.astype(narrow), row, axis=0, tiled=True)
    act_wide = act_half.astype(wide)
    act_sq = (act_wide * act_wide).astype(narrow)

    summed_t = scatter_sum(contract(act_sq, grad_sq, 0, 0), "x")
    summed_t = lax.optimization_barrier(summed_t)
    spread_t = token_count * (summed_t / token_count + damping)
    scaled_t = (eigen_noise.T * lax.rsqrt(spread_t)).astype(narrow)
    scaled_t, summed_t = lax.optimization_barrier((scaled_t, summed_t))
    scales = (summed_t / token_count).T
    widened_t = spread(scaled_t, "x")

    hidden = scatter_sum(contract(act_half, widened_t, 1, 0), ("tok", "yl")).astype(narrow)
    hidden = spread(hidden, col)
    halves = pair_sum(contract(hidden, grad_basis, 1, 1), "core")
    shift = scatter_sum(halves, "yh")[0].astype(narrow)
    output_shift = lax.all_gather(shift, row, axis=0, tiled=True)
    return (scales, output_shift)


def solution(mesh):
    fine = Mesh(mesh.devices.reshape(8, 4, 2, 4, 2), ("tok", "yh", "core", "x", "yl"))
    in_specs = (
        P("tok", row),
        P("tok", col),
        P(row, ("tok", *col)),
        P(col, row),
        P(row, ("tok", *col)),
    )
    out_specs = (P(row, ("tok", *col)), P("tok", col))
    return jax.shard_map(plan, mesh=fine, in_specs=in_specs, out_specs=out_specs, check_vma=False)
```

```python
import jax
import jax.numpy as jnp
from jax import lax
from jax.experimental import pallas as pl
from jax.experimental.layout import Layout, with_layout_constraint
from jax.experimental.pallas import tpu as pltpu
from jax.sharding import Mesh, PartitionSpec as P

damping = 0.1
narrow = jnp.bfloat16
wide = jnp.float32
row = ("yh", "core")
col = ("x", "yl")


def contract(former, latter, former_dim, latter_dim):
    return lax.dot_general(
        former,
        latter,
        (((former_dim,), (latter_dim,)), ((), ())),
        preferred_element_type=wide,
    )


def exchange(blocks, axes):
    return lax.all_to_all(blocks, axes, 0, 0, tiled=True)


def spread(block, axes):
    members = lax.axis_size(axes)
    copies = jnp.broadcast_to(block[None], (members, *block.shape))
    return exchange(copies.reshape(members * block.shape[0], *block.shape[1:]), axes)


def copy_block(place_ref, rows_ref, copy_ref):
    copy_ref[0] = rows_ref[...]


def copies_of_slab(rows, place, slab, copies):
    width = rows.shape[1]
    out = pl.pallas_call(
        copy_block,
        grid_spec=pltpu.PrefetchScalarGridSpec(
            num_scalar_prefetch=1,
            grid=(copies,),
            in_specs=[pl.BlockSpec((slab, width), lambda step, place_ref: (place_ref[0], 0))],
            out_specs=pl.BlockSpec((1, slab, width), lambda step, place_ref: (step, 0, 0)),
        ),
        out_shape=jax.ShapeDtypeStruct((copies, slab, width), rows.dtype),
        cost_estimate=pl.CostEstimate(flops=0, bytes_accessed=2 * copies * slab * width, transcendentals=0),
    )(place.reshape(1).astype(jnp.int32), rows)
    return out.reshape(copies * slab, width)


def scatter_sum(partial, axes):
    members = lax.axis_size(axes)
    parts = exchange(partial.astype(narrow), axes)
    parts = parts.reshape(members, parts.shape[0] // members, *parts.shape[1:])
    return jnp.sum(parts.astype(wide), axis=0)


def pick(blocks, index, axis):
    return lax.dynamic_index_in_dim(blocks, index, axis, keepdims=False)


def shifted(block, axis, step):
    members = lax.axis_size(axis)
    return lax.ppermute(block, axis, [(i, (i + step) % members) for i in range(members)])


def pair_sum(partial, axis):
    half = partial.reshape(4, 2, partial.shape[0] // 8, partial.shape[1])
    mine = lax.axis_index(axis)
    sent, kept = lax.optimization_barrier((pick(half, 1 - mine, 1).astype(narrow), pick(half, mine, 1)))
    return kept + pick(lax.all_gather(sent, axis), 1 - mine, 0).astype(wide)


def ring_sum(blocks, axis):
    mine = lax.axis_index(axis)
    members = lax.axis_size(axis)
    total = pick(blocks, mine, 0).astype(wide)
    for step in sorted(range(1, members), key=lambda step: abs(2 * step - members)):
        total = total + shifted(pick(blocks, (mine + step) % members, 0), axis, step).astype(wide)
    return total


def plan(activations, gradients, act_basis, grad_basis, eigen_noise):
    token_count = activations.shape[0] * lax.axis_size("tok")
    slab = activations.shape[0] // lax.axis_size("x")

    act_rows = exchange(copies_of_slab(activations, lax.axis_index("x"), slab, lax.axis_size("tok")), "tok")
    grad_part = contract(gradients, grad_basis, 1, 0).astype(narrow)
    grad_part = grad_part.reshape(-1, slab, grad_part.shape[1])
    own_basis_t = with_layout_constraint(act_basis.T, Layout((0, 1)))
    basis_t = lax.all_gather(own_basis_t, "x", axis=0, tiled=True)
    grad_half = ring_sum(grad_part, "x")
    grad_proj = grad_half + shifted(grad_half.astype(narrow), "yl", 1).astype(wide)
    grad_sq = (grad_proj * grad_proj).astype(narrow)

    act_halves = pair_sum(contract(act_rows, basis_t, 1, 1), "core")
    act_proj = scatter_sum(act_halves, "yh")[0]
    grad_sq = lax.all_gather(grad_sq, "tok", axis=0, tiled=True)
    act_half = lax.all_gather(act_proj.astype(narrow), row, axis=0, tiled=True)
    act_wide = act_half.astype(wide)
    act_sq = (act_wide * act_wide).astype(narrow)

    summed_t = scatter_sum(contract(act_sq, grad_sq, 0, 0), "x")
    summed_t = lax.optimization_barrier(summed_t)
    spread_t = token_count * (summed_t / token_count + damping)
    scaled_t = (eigen_noise.T * lax.rsqrt(spread_t)).astype(narrow)
    scaled_t, summed_t = lax.optimization_barrier((scaled_t, summed_t))
    scales = (summed_t / token_count).T
    widened_t = spread(scaled_t, "x")

    hidden = scatter_sum(contract(act_half, widened_t, 1, 0), ("tok", "yl")).astype(narrow)
    hidden = spread(hidden, col)
    halves = pair_sum(contract(hidden, grad_basis, 1, 1), "core")
    shift = scatter_sum(halves, "yh")[0].astype(narrow)
    output_shift = lax.all_gather(shift, row, axis=0, tiled=True)
    return (scales, output_shift)


def solution(mesh):
    fine = Mesh(mesh.devices.reshape(8, 4, 2, 4, 2), ("tok", "yh", "core", "x", "yl"))
    in_specs = (
        P("tok", row),
        P("tok", col),
        P(row, ("tok", *col)),
        P(col, row),
        P(row, ("tok", *col)),
    )
    out_specs = (P(row, ("tok", *col)), P("tok", col))
    return jax.shard_map(plan, mesh=fine, in_specs=in_specs, out_specs=out_specs, check_vma=False)
```

```python
import jax
import jax.numpy as jnp
from jax import lax
from jax.experimental.layout import Layout, with_layout_constraint
from jax.sharding import Mesh, PartitionSpec as P

damping = 0.1
narrow = jnp.bfloat16
wide = jnp.float32
row = ("yh", "core")
col = ("x", "yl")


def contract(former, latter, former_dim, latter_dim):
    return lax.dot_general(
        former,
        latter,
        (((former_dim,), (latter_dim,)), ((), ())),
        preferred_element_type=wide,
    )


def exchange(blocks, axes):
    return lax.all_to_all(blocks, axes, 0, 0, tiled=True)


def spread(block, axes):
    members = lax.axis_size(axes)
    copies = jnp.broadcast_to(block[None], (members, *block.shape))
    return exchange(copies.reshape(members * block.shape[0], *block.shape[1:]), axes)


def scatter_sum(partial, axes):
    members = lax.axis_size(axes)
    parts = exchange(partial.astype(narrow), axes)
    parts = parts.reshape(members, parts.shape[0] // members, *parts.shape[1:])
    return jnp.sum(parts.astype(wide), axis=0)


def pick(blocks, index, axis):
    return lax.dynamic_index_in_dim(blocks, index, axis, keepdims=False)


def shifted(block, axis, step):
    members = lax.axis_size(axis)
    return lax.ppermute(block, axis, [(i, (i + step) % members) for i in range(members)])


def pair_sum(partial, axis):
    half = partial.reshape(4, 2, partial.shape[0] // 8, partial.shape[1])
    mine = lax.axis_index(axis)
    sent, kept = lax.optimization_barrier((pick(half, 1 - mine, 1).astype(narrow), pick(half, mine, 1)))
    return kept + pick(lax.all_gather(sent, axis), 1 - mine, 0).astype(wide)


def ring_sum(blocks, axis):
    mine = lax.axis_index(axis)
    members = lax.axis_size(axis)
    total = pick(blocks, mine, 0).astype(wide)
    for step in sorted(range(1, members), key=lambda step: abs(2 * step - members)):
        total = total + shifted(pick(blocks, (mine + step) % members, 0), axis, step).astype(wide)
    return total


def plan(activations, gradients, act_basis, grad_basis, eigen_noise):
    token_count = activations.shape[0] * lax.axis_size("tok")
    slab = activations.shape[0] // lax.axis_size("x")

    own_rows = lax.dynamic_slice_in_dim(activations, lax.axis_index("x") * slab, slab, 0)
    act_rows = spread(own_rows, "tok")
    grad_part = contract(gradients, grad_basis, 1, 0).astype(narrow)
    grad_part = grad_part.reshape(-1, slab, grad_part.shape[1])
    basis = lax.all_gather(act_basis, "x", axis=1, tiled=True)
    grad_half = ring_sum(grad_part, "x")
    grad_proj = grad_half + shifted(grad_half.astype(narrow), "yl", 1).astype(wide)
    grad_sq = (grad_proj * grad_proj).astype(narrow)

    act_halves = pair_sum(contract(act_rows, basis, 1, 0), "core")
    act_proj = scatter_sum(act_halves, "yh")[0]
    grad_sq = lax.all_gather(grad_sq, "tok", axis=0, tiled=True)
    act_half = lax.all_gather(act_proj.astype(narrow), row, axis=0, tiled=True)
    act_wide = act_half.astype(wide)
    act_sq_t = with_layout_constraint((act_wide * act_wide).astype(narrow).T, Layout((0, 1)))
    act_sq_t = lax.optimization_barrier(act_sq_t)

    summed_t = scatter_sum(contract(act_sq_t, grad_sq, 1, 0), "x")
    summed_t = lax.optimization_barrier(summed_t)
    spread_t = token_count * (summed_t / token_count + damping)
    scaled_t = (eigen_noise.T * lax.rsqrt(spread_t)).astype(narrow)
    scaled_t, summed_t = lax.optimization_barrier((scaled_t, summed_t))
    scales = (summed_t / token_count).T
    widened_t = spread(scaled_t, "x")

    hidden = scatter_sum(contract(act_half, widened_t, 1, 0), ("tok", "yl")).astype(narrow)
    hidden = spread(hidden, col)
    halves = pair_sum(contract(hidden, grad_basis, 1, 1), "core")
    shift = scatter_sum(halves, "yh")[0].astype(narrow)
    output_shift = lax.all_gather(shift, row, axis=0, tiled=True)
    return (scales, output_shift)


def solution(mesh):
    fine = Mesh(mesh.devices.reshape(8, 4, 2, 4, 2), ("tok", "yh", "core", "x", "yl"))
    in_specs = (
        P("tok", row),
        P("tok", col),
        P(row, ("tok", *col)),
        P(col, row),
        P(row, ("tok", *col)),
    )
    out_specs = (P(row, ("tok", *col)), P("tok", col))
    return jax.shard_map(plan, mesh=fine, in_specs=in_specs, out_specs=out_specs, check_vma=False)
```

```python
import jax
import jax.numpy as jnp
from jax import lax
from jax.sharding import Mesh, PartitionSpec as P

damping = 0.1
narrow = jnp.bfloat16
wide = jnp.float32
row = ("yh", "core")
col = ("x", "yl")


def contract(former, latter, former_dim, latter_dim):
    return lax.dot_general(
        former,
        latter,
        (((former_dim,), (latter_dim,)), ((), ())),
        preferred_element_type=wide,
    )


def exchange(blocks, axes):
    return lax.all_to_all(blocks, axes, 0, 0, tiled=True)


def spread(block, axes):
    members = lax.axis_size(axes)
    copies = jnp.broadcast_to(block[None], (members, *block.shape))
    return exchange(copies.reshape(members * block.shape[0], *block.shape[1:]), axes)


def scatter_sum(partial, axes):
    members = lax.axis_size(axes)
    parts = exchange(partial.astype(narrow), axes)
    parts = parts.reshape(members, parts.shape[0] // members, *parts.shape[1:])
    return jnp.sum(parts.astype(wide), axis=0)


def pick(blocks, index, axis):
    return lax.dynamic_index_in_dim(blocks, index, axis, keepdims=False)


def shifted(block, axis, step):
    members = lax.axis_size(axis)
    return lax.ppermute(block, axis, [(i, (i + step) % members) for i in range(members)])


def pair_sum(partial, axis):
    half = partial.reshape(4, 2, partial.shape[0] // 8, partial.shape[1])
    mine = lax.axis_index(axis)
    sent, kept = lax.optimization_barrier((pick(half, 1 - mine, 1).astype(narrow), pick(half, mine, 1)))
    return kept + pick(lax.all_gather(sent, axis), 1 - mine, 0).astype(wide)


def columns_of_pair(act_half):
    half = act_half.reshape(8, 2, act_half.shape[0] // 16, act_half.shape[1])
    mine = lax.axis_index("yl")
    theirs = shifted(pick(half, 1 - mine, 1), "yl", 1)
    kept = pick(half, mine, 1)
    pair = (lax.select_n(mine, kept, theirs), lax.select_n(mine, theirs, kept))
    blocks = [side.reshape(-1, 4, 1, side.shape[-1] // 4) for side in pair]
    return lax.optimization_barrier(jnp.concatenate(blocks, axis=2).reshape(-1, 2 * act_half.shape[1]))


def ring_sum(blocks, axis):
    mine = lax.axis_index(axis)
    members = lax.axis_size(axis)
    total = pick(blocks, mine, 0).astype(wide)
    for step in sorted(range(1, members), key=lambda step: abs(2 * step - members)):
        total = total + shifted(pick(blocks, (mine + step) % members, 0), axis, step).astype(wide)
    return total


def plan(activations, gradients, act_basis, grad_basis, eigen_noise):
    token_count = activations.shape[0] * lax.axis_size("tok")
    slab = activations.shape[0] // lax.axis_size("x")

    own_rows = lax.dynamic_slice_in_dim(activations, lax.axis_index("x") * slab, slab, 0)
    act_rows = spread(own_rows, "tok")
    grad_part = contract(gradients, grad_basis, 1, 0).astype(narrow)
    grad_part = grad_part.reshape(-1, slab, grad_part.shape[1])
    basis = lax.all_gather(act_basis, "x", axis=1, tiled=True)
    grad_half = ring_sum(grad_part, "x")
    grad_proj = grad_half + shifted(grad_half.astype(narrow), "yl", 1).astype(wide)
    grad_sq = (grad_proj * grad_proj).astype(narrow)

    act_halves = pair_sum(contract(act_rows, basis, 1, 0), "core")
    act_proj = scatter_sum(act_halves, "yh")[0]
    grad_sq = lax.all_gather(grad_sq, "tok", axis=0, tiled=True)
    act_half = lax.all_gather(act_proj.astype(narrow), row, axis=0, tiled=True)
    act_wide = act_half.astype(wide)
    act_sq = (act_wide * act_wide).astype(narrow)

    act_cols = columns_of_pair(act_half)

    summed_t = scatter_sum(contract(act_sq, grad_sq, 0, 0), "x")
    summed_t = lax.optimization_barrier(summed_t)
    spread_t = token_count * (summed_t / token_count + damping)
    scaled_t = (eigen_noise.T * lax.rsqrt(spread_t)).astype(narrow)
    scaled_t, summed_t = lax.optimization_barrier((scaled_t, summed_t))
    scales = (summed_t / token_count).T
    widened_t = spread(scaled_t, col)

    hidden = scatter_sum(contract(act_cols, widened_t, 1, 0), "tok").astype(narrow)
    hidden = spread(hidden, col)
    halves = pair_sum(contract(hidden, grad_basis, 1, 1), "core")
    shift = scatter_sum(halves, "yh")[0].astype(narrow)
    output_shift = lax.all_gather(shift, row, axis=0, tiled=True)
    return (scales, output_shift)


def solution(mesh):
    fine = Mesh(mesh.devices.reshape(8, 4, 2, 4, 2), ("tok", "yh", "core", "x", "yl"))
    in_specs = (
        P("tok", row),
        P("tok", col),
        P(row, ("tok", *col)),
        P(col, row),
        P(row, ("tok", *col)),
    )
    out_specs = (P(row, ("tok", *col)), P("tok", col))
    return jax.shard_map(plan, mesh=fine, in_specs=in_specs, out_specs=out_specs, check_vma=False)
```

```python
import jax
import jax.numpy as jnp
from jax import lax
from jax.sharding import Mesh, PartitionSpec as P

damping = 0.1
narrow = jnp.bfloat16
wide = jnp.float32
row = ("yh", "core")
col = ("x", "yl")


def contract(former, latter, former_dim, latter_dim):
    return lax.dot_general(
        former,
        latter,
        (((former_dim,), (latter_dim,)), ((), ())),
        preferred_element_type=wide,
    )


def exchange(blocks, axes):
    return lax.all_to_all(blocks, axes, 0, 0, tiled=True)


def spread(block, axes):
    members = lax.axis_size(axes)
    copies = jnp.broadcast_to(block[None], (members, *block.shape))
    return exchange(copies.reshape(members * block.shape[0], *block.shape[1:]), axes)


def scatter_sum(partial, axes):
    members = lax.axis_size(axes)
    parts = exchange(partial.astype(narrow), axes)
    parts = parts.reshape(members, parts.shape[0] // members, *parts.shape[1:])
    return jnp.sum(parts.astype(wide), axis=0)


def pick(blocks, index, axis):
    return lax.dynamic_index_in_dim(blocks, index, axis, keepdims=False)


def shifted(block, axis, step):
    members = lax.axis_size(axis)
    return lax.ppermute(block, axis, [(i, (i + step) % members) for i in range(members)])


def pair_sum(partial, axis):
    half = partial.reshape(4, 2, partial.shape[0] // 8, partial.shape[1])
    mine = lax.axis_index(axis)
    sent, kept = lax.optimization_barrier((pick(half, 1 - mine, 1).astype(narrow), pick(half, mine, 1)))
    return kept + pick(lax.all_gather(sent, axis), 1 - mine, 0).astype(wide)


def ring_sum(blocks, axis):
    mine = lax.axis_index(axis)
    members = lax.axis_size(axis)
    total = pick(blocks, mine, 0).astype(wide)
    for step in sorted(range(1, members), key=lambda step: abs(2 * step - members)):
        total = total + shifted(pick(blocks, (mine + step) % members, 0), axis, step).astype(wide)
    return total


def plan(activations, gradients, act_basis, grad_basis, eigen_noise):
    token_count = activations.shape[0] * lax.axis_size("tok")
    slab = activations.shape[0] // lax.axis_size("x")

    own_rows = lax.dynamic_slice_in_dim(activations, lax.axis_index("x") * slab, slab, 0)
    act_rows = spread(own_rows, "tok")
    grad_part = contract(gradients, grad_basis, 1, 0).astype(narrow)
    grad_part = grad_part.reshape(-1, slab, grad_part.shape[1])
    basis = lax.all_gather(act_basis, "x", axis=1, tiled=True)
    grad_half = ring_sum(grad_part, "x")
    both = lax.all_gather(grad_half.astype(narrow), "yl")
    grad_proj = grad_half + pick(both, 1 - lax.axis_index("yl"), 0).astype(wide)
    grad_sq = (grad_proj * grad_proj).astype(narrow)

    act_halves = pair_sum(contract(act_rows, basis, 1, 0), "core")
    act_proj = scatter_sum(act_halves, "yh")[0]
    grad_sq = lax.all_gather(grad_sq, "tok", axis=0, tiled=True)
    act_half = lax.all_gather(act_proj.astype(narrow), row, axis=0, tiled=True)
    act_wide = act_half.astype(wide)
    act_sq = (act_wide * act_wide).astype(narrow)

    scales_t = scatter_sum(contract(act_sq, grad_sq, 0, 0), "x") / token_count
    scaled_t = (eigen_noise.T * lax.rsqrt(token_count * (scales_t + damping))).astype(narrow)
    widened_t = spread(scaled_t, "x")

    hidden = scatter_sum(contract(act_half, widened_t, 1, 0), ("tok", "yl")).astype(narrow)
    hidden = spread(hidden, col)
    halves = pair_sum(contract(hidden, grad_basis, 1, 1), "core")
    shift = scatter_sum(halves, "yh")[0].astype(narrow)
    output_shift = lax.all_gather(shift, row, axis=0, tiled=True)
    return (scales_t.T, output_shift)


def solution(mesh):
    fine = Mesh(mesh.devices.reshape(8, 4, 2, 4, 2), ("tok", "yh", "core", "x", "yl"))
    in_specs = (
        P("tok", row),
        P("tok", col),
        P(row, ("tok", *col)),
        P(col, row),
        P(row, ("tok", *col)),
    )
    out_specs = (P(row, ("tok", *col)), P("tok", col))
    return jax.shard_map(plan, mesh=fine, in_specs=in_specs, out_specs=out_specs, check_vma=False)
```
